32 devices in a mesh: row: 4 (over x, core), col: 8 (over z, y).
Axes of the slice: x: 2, y: 2, z: 4, core: 2. Of those that a mesh axis runs over, the one named last changes fastest.
Arguments:
- markov: bfloat16 [2, 256, 128, 128], P(None, 'col'), may hold values from -6 to 6
- omega: bfloat16 [32768, 64], P('col'), may hold values from -0.03125 to 0.03125
Outputs:
- denoised: float32 [2, 256, 128, 128], P(None, 'col')
The draws below stay inside these ranges and needn't reach their ends.
All inputs are finite; a program needn't handle non-finite values.
Results may differ from the reference program's by a relative error of at most 0.0007.
Values may be sent and summed in bfloat16 or wider, within the bound.
No kernel may reach another device: no remote copies, remote signals or barrier semaphores. Data moves between devices by JAX's collectives and lax.ppermute only.
A program may use at most 64 MiB of HBM per device.

```python
import jax
import jax.numpy as jnp
from jax import lax

P_SIZE = 128
M = 128
K = 64
NS_STEPS = 8
NBR = 128
NBC = 256
COLS = 32768


def draw_markov(key, part):
    keys = jax.random.split(key, 5)
    modes = K // 2
    lag_pos = jnp.arange(2 * NBC, dtype=jnp.float32)
    radius = jnp.exp(-jax.random.uniform(keys[0], (modes,), jnp.float32, 0.0, 2.5) / (2 * NBC))
    freqs = jax.random.uniform(keys[1], (modes,), jnp.float32, 0.05, 3.0)
    left = jax.random.normal(keys[2], (2, P_SIZE, modes), jnp.float32) / jnp.sqrt(1.0 * modes)
    right = jax.random.normal(keys[3], (2, modes, M), jnp.float32)
    envelope = radius[None, :] ** lag_pos[:, None]
    cosine = envelope * jnp.cos(freqs[None, :] * lag_pos[:, None])
    sine = envelope * jnp.sin(freqs[None, :] * lag_pos[:, None])
    signal = jnp.einsum('pr,lr,rm->lpm', left[0], cosine, right[0]) + jnp.einsum('pr,lr,rm->lpm', left[1], sine, right[1])
    noise = 0.3 * jax.random.normal(keys[4], (2 * NBC, P_SIZE, M), jnp.float32)
    return jnp.clip(signal + noise, -6.0, 6.0).reshape(2, NBC, P_SIZE, M).astype(jnp.bfloat16)


def levels(stream_key, dims, cuts, least, top_value):
    gain = 1.0
    for position, blocks in cuts:
        steps = jax.random.uniform(jax.random.fold_in(jax.random.fold_in(stream_key, 6), position), (blocks,), jnp.float32, least / len(cuts), top_value / len(cuts))
        gain = gain * jnp.repeat(jnp.exp(steps), dims[position] // blocks).reshape((-1,) + (1,) * (len(dims) - 1 - position))
    return gain


def gaussian(rng, shape, spread, limit, pieces=(), kind=jnp.bfloat16):
    array = jax.random.normal(rng, shape, jnp.float32) * spread
    if len(pieces) > 0:
        array = levels(rng, shape, pieces, -0.22, 0.18) * array
    return jnp.clip(array, min=-limit, max=limit).astype(kind)


def setup_inputs(seed: int = 0) -> dict:
    streams_of = jax.random.split(jax.random.key(seed), 3)
    return {
        "markov": draw_markov(jax.random.fold_in(streams_of[2], 71), 0),
        "omega": gaussian(streams_of[1], (COLS, K), COLS ** -0.5, 0.03125, ((0, 8),)),
    }


norm_floor = 1e-06

def reference(markov, omega):
    lag_blocks = markov.reshape(2 * NBC, P_SIZE, M).astype(jnp.float32)
    omega_blocks = omega.reshape(NBC, M, K).astype(jnp.float32)
    column_ids = jnp.arange(NBC, dtype=jnp.int32)

    def range_step(running, column_id):
        window = lax.dynamic_slice_in_dim(lag_blocks, column_id, NBR, 0)
        weights = lax.dynamic_index_in_dim(omega_blocks, column_id, 0, keepdims=False)
        return (running + jnp.einsum('ipm,mk->ipk', window, weights), None)
    sketch, _ = lax.scan(range_step, jnp.zeros((NBR, P_SIZE, K), jnp.float32), column_ids)
    sketch = sketch.reshape(NBR * P_SIZE, K)
    gram = jnp.dot(sketch.T, sketch, precision=lax.Precision.HIGHEST, preferred_element_type=jnp.float32)
    current = sketch / jnp.sqrt(jnp.trace(gram) + norm_floor)
    for sweep in range(NS_STEPS):
        inner = jnp.dot(current.T, current, precision=lax.Precision.HIGHEST, preferred_element_type=jnp.float32)
        current = 1.5 * current - 0.5 * jnp.dot(current, inner, precision=lax.Precision.HIGHEST, preferred_element_type=jnp.float32)
    basis = current.astype(jnp.bfloat16)
    basis_f = basis.astype(jnp.float32).reshape(NBR, P_SIZE, K)

    def projection_update(carry, column_id):
        window = lax.dynamic_slice_in_dim(lag_blocks, column_id, NBR, 0)
        return (carry, jnp.einsum('ipk,ipm->km', basis_f, window))
    _, projected_matrix = lax.scan(projection_update, 0.0, column_ids)
    projected_matrix = projected_matrix.astype(jnp.bfloat16)
    projected_matrix = lax.optimization_barrier(projected_matrix).astype(jnp.float32)

    def lag_step(running, inputs):
        row_position, orthonormal_row_vector = inputs
        summand_terms = jnp.einsum('fb,gby->gfy', orthonormal_row_vector, projected_matrix)
        current_sum = lax.dynamic_slice_in_dim(running, row_position, NBC, 0)
        return (lax.dynamic_update_slice_in_dim(running, current_sum + summand_terms, row_position, 0), None)
    totals, _ = lax.scan(lag_step, jnp.zeros((NBR + NBC, P_SIZE, M), jnp.float32), (jnp.arange(NBR, dtype=jnp.int32), basis_f))
    totals = jnp.pad(totals, ((0, 2 * NBC - NBR - NBC), (0, 0), (0, 0)))
    lag_ids = jnp.arange(2 * NBC, dtype=jnp.int32)
    counts = jnp.maximum(jnp.minimum(lag_ids, NBR - 1) - jnp.maximum(0, lag_ids - NBC + 1) + 1, 0)
    counts_f = counts.astype(jnp.float32)[:, None, None]
    averaged = totals / jnp.maximum(counts_f, 1.0)
    merged = jnp.where(counts_f > 0, 0.5 * lag_blocks + 0.5 * averaged, lag_blocks)
    return merged.reshape(2, NBC, P_SIZE, M)
```

```python
import functools

import jax
import jax.numpy as jnp
from jax import lax
from jax.experimental import pallas as pl
from jax.experimental.pallas import tpu as pltpu
from jax.sharding import PartitionSpec as P

NS_STEPS = 8
norm_floor = 1e-06
SHARE = 0.375
F32 = jnp.float32
BF16 = jnp.bfloat16
HIGHEST = lax.Precision.HIGHEST
VMEM_LIMIT = 56 * 1024 * 1024

NT = (((1,), (1,)), ((), ()))
NN = (((1,), (0,)), ((), ()))


def matmul(left, right, dims=NN):
    return lax.dot_general(left, right, dims, preferred_element_type=F32)


def shift_col(x, distance):
    n = lax.axis_size("col")
    return lax.ppermute(x, "col", [(i, (i + distance) % n) for i in range(n)])


def swap_row(x, bit):
    n = lax.axis_size("row")
    return lax.ppermute(x, "row", [(i, i ^ bit) for i in range(n)])


def gather_row(x):
    pieces, offsets = [x], [0]
    bit = lax.axis_size("row") // 2
    while bit:
        pieces = pieces + [swap_row(p, bit) for p in pieces]
        offsets = offsets + [o ^ bit for o in offsets]
        bit //= 2
    return pieces, offsets


def sketch_kernel(count, half_ref, lag_ref, *refs):
    w_refs, out_ref, lags, acc, sems = refs[:count], refs[count], refs[count + 1], refs[count + 2], refs[count + 3]
    blocks = lag_ref.shape[1]
    pairs, kk, _ = w_refs[0].shape
    rows = out_ref.shape[0]
    copies = [
        pltpu.make_async_copy(lag_ref.at[h], lags.at[h, pl.ds(1, blocks)], sems.at[h]) for h in range(2)
    ]
    for copy in copies:
        copy.start()
    zero = jnp.zeros(lags.shape[2:], BF16)
    for h in range(2):
        lags[h, 0] = zero
        lags[h, blocks + 1] = zero
        lags[h, blocks + 2] = zero
    acc[...] = jnp.zeros_like(acc)
    for copy in copies:
        copy.wait()

    def step(t, carry):
        for e in range(count):
            h = half_ref[e]
            before, here, after = lags[h, 2 * t], lags[h, 2 * t + 1], lags[h, 2 * t + 2]
            tile = jnp.concatenate(
                [jnp.concatenate([before, here], 1), jnp.concatenate([here, after], 1)], 0
            )
            part = matmul(w_refs[e][...].reshape(pairs * kk, 256), tile, NT)
            acc[pl.ds(pairs * (e + 1) - t, pairs)] += part.reshape(pairs, kk, 256)
        return carry

    lax.fori_loop(0, pairs + 1, step, 0)

    def store(q, carry):
        out_ref[2 * q] = acc[q + pairs, :, :128].astype(BF16)
        out_ref[2 * q + 1] = acc[q + pairs + 1, :, 128:].astype(BF16)
        return carry

    lax.fori_loop(0, rows // 2, store, 0)


def sketch_part(halves, markov, w_blocks, rows):
    count = len(w_blocks)
    blocks = markov.shape[1]
    pairs, kk, _ = w_blocks[0].shape
    return pl.pallas_call(
        functools.partial(sketch_kernel, count),
        out_shape=jax.ShapeDtypeStruct((rows, kk, 128), BF16),
        in_specs=[pl.BlockSpec(memory_space=pltpu.SMEM), pl.BlockSpec(memory_space=pl.ANY)]
        + [pl.BlockSpec(memory_space=pltpu.VMEM)] * count,
        out_specs=pl.BlockSpec(memory_space=pltpu.VMEM),
        scratch_shapes=[
            pltpu.VMEM((2, blocks + 3, 128, 128), BF16),
            pltpu.VMEM((pairs * (count + 1), kk, 256), F32),
            pltpu.SemaphoreType.DMA((2,)),
        ],
        compiler_params=pltpu.CompilerParams(vmem_limit_bytes=VMEM_LIMIT),
        name="sketch",
    )(halves, markov, *w_blocks)


def split(x):
    high = x.astype(BF16)
    return high, (x - high.astype(F32)).astype(BF16)


def full_dot(left, right):
    return jnp.dot(left, right, precision=HIGHEST, preferred_element_type=F32)


def newton_schulz(gram):
    size = gram.shape[0]
    row = lax.broadcasted_iota(jnp.int32, (size, size), 0)
    col = lax.broadcasted_iota(jnp.int32, (size, size), 1)
    eye = jnp.where(row == col, 1.0, 0.0)
    scale = 1.0 / jnp.sqrt(jnp.sum(gram * eye, keepdims=True) + norm_floor)
    inner = gram * (scale * scale)
    coeffs = eye * scale
    for sweep in range(NS_STEPS):
        update = 1.5 * eye - 0.5 * inner
        coeffs = full_dot(coeffs, update)
        if sweep + 1 < NS_STEPS:
            inner = full_dot(full_dot(inner, update), update)
    return coeffs


def needed(half_ref, count, pairs, h, g):
    first = (2 * g) // pairs
    second = jnp.minimum(first + 1, count - 1)
    return jnp.logical_or(half_ref[first] == h, half_ref[second] == h)


def basis_tile(basis_ref, g, rank):
    step = 256 // rank
    low = pl.multiple_of(g * (step * rank), 64)
    return jnp.concatenate(
        [basis_ref[pl.ds(low + rank, 256), :], basis_ref[pl.ds(low, 256), :]], 1
    )


def project_kernel(count, pieces, half_ref, *refs):
    s_refs = refs[:pieces]
    lt_ref, basis_ref, out_ref, sketch, acc = refs[pieces:]
    rows, kk, _ = s_refs[0].shape
    rank = kk * pieces
    group = 256 // rank
    _, pairs, mm, _ = out_ref.shape
    groups = rows // group

    def load(g, gram):
        block = jnp.concatenate(
            [s_refs[j][group * g + i] for i in range(group) for j in range(pieces)], 0
        )
        sketch[pl.ds(pl.multiple_of(g * 256, 256), 256), :] = block
        return gram + matmul(block, block, NT)

    gram4 = lax.fori_loop(0, groups, load, jnp.zeros((256, 256), F32))
    gram = sum(
        gram4[rank * i : rank * (i + 1), rank * i : rank * (i + 1)] for i in range(group)
    )
    coeffs = newton_schulz(gram)
    wide = jnp.concatenate([coeffs] * group, 1)
    wide = jnp.concatenate([wide] * group, 0)
    row = lax.broadcasted_iota(jnp.int32, (256, 256), 0) // rank
    col = lax.broadcasted_iota(jnp.int32, (256, 256), 1) // rank
    wide = jnp.where(row == col, wide, 0.0)
    high, low = split(wide)

    basis_ref[pl.ds(0, 2 * rank), :] = jnp.zeros((2 * rank, 128), BF16)
    basis_ref[pl.ds((rows + 2) * rank, 3 * rank), :] = jnp.zeros((3 * rank, 128), BF16)

    def rotate(g, carry):
        block = sketch[pl.ds(pl.multiple_of(g * 256, 256), 256), :]
        value = matmul(high, block) + matmul(low, block)
        basis_ref[pl.ds(pl.multiple_of(g * 256 + 2 * rank, 64), 256), :] = value.astype(BF16)
        return carry

    lax.fori_loop(0, groups, rotate, 0)
    acc[...] = jnp.zeros_like(acc)

    def step(g, carry):
        tile = basis_tile(basis_ref, g, rank)
        for h in range(2):

            @pl.when(needed(half_ref, count, pairs, h, g))
            def _():
                part = matmul(lt_ref[h], tile, NT)
                acc[h, pl.ds(2 * g + 1, pairs)] += part.reshape(pairs, mm, 256)

        return carry

    lax.fori_loop(0, groups + 1, step, 0)
    for e in range(count):
        h = half_ref[e]
        here = acc[h, pl.ds(pairs * e + 1, pairs), :, :128]
        before = acc[h, pl.ds(pairs * e, pairs), :, 128:]
        out_ref[e] = (here + before).astype(BF16)


def project(halves, sketches, lag_t, count):
    pieces = len(sketches)
    rows, kk, _ = sketches[0].shape
    rank = kk * pieces
    mm = 128 // pieces
    pairs = lag_t.shape[1] // mm
    return pl.pallas_call(
        functools.partial(project_kernel, count, pieces),
        out_shape=[
            jax.ShapeDtypeStruct(((rows + 5) * rank, 128), BF16),
            jax.ShapeDtypeStruct((count, pairs, mm, 128), BF16),
        ],
        in_specs=[pl.BlockSpec(memory_space=pltpu.SMEM)]
        + [pl.BlockSpec(memory_space=pltpu.VMEM)] * (pieces + 1),
        out_specs=[pl.BlockSpec(memory_space=pltpu.VMEM)] * 2,
        scratch_shapes=[
            pltpu.VMEM((rows * rank, 128), BF16),
            pltpu.VMEM((2, pairs * count + 1, mm, 256), F32),
        ],
        compiler_params=pltpu.CompilerParams(vmem_limit_bytes=VMEM_LIMIT),
        name="project",
    )(halves, *sketches, lag_t)


def totals_kernel(count, half_ref, *refs):
    p_refs = refs[:count]
    basis_ref, lt_ref, inv_ref, out_ref, wide, acc = refs[count:]
    pairs, mm, _ = p_refs[0].shape
    span = pairs * mm
    groups = inv_ref.shape[0] and (basis_ref.shape[0] // 64 - 5) // 4
    for h in range(2):
        wide[h, pl.ds(count * span - mm, mm), 128:] = jnp.zeros((mm, 128), BF16)
    for e in range(count):
        block = p_refs[e][...].reshape(span, 128)
        zero = jnp.zeros_like(block)
        for h in range(2):
            kept = jnp.where(half_ref[e] == h, block, zero)
            wide[h, pl.ds(e * span, span), :128] = kept
            if e == 0:
                wide[h, pl.ds(0, span - mm), 128:] = kept[mm:]
            else:
                wide[h, pl.ds(e * span - mm, span), 128:] = kept
    acc[...] = jnp.zeros_like(acc)

    def step(g, carry):
        tile = basis_tile(basis_ref, g, 64)
        for h in range(2):

            @pl.when(needed(half_ref, count, pairs, h, g))
            def _():
                rows = wide[h, pl.ds(pl.multiple_of(g * 2 * mm, 32), span), :]
                acc[h] += matmul(rows, tile)

        return carry

    lax.fori_loop(0, groups + 1, step, 0)
    for h in range(2):
        scaled = acc[h].reshape(pairs, mm, 256) * inv_ref[h]
        out_ref[h] = (scaled.reshape(span, 256) - SHARE * lt_ref[h].astype(F32)).astype(BF16)


def totals(halves, p_blocks, basis, lag_t, inverse):
    count = len(p_blocks)
    pairs, mm, _ = p_blocks[0].shape
    span = pairs * mm
    return pl.pallas_call(
        functools.partial(totals_kernel, count),
        out_shape=jax.ShapeDtypeStruct((2, span, 256), BF16),
        in_specs=[pl.BlockSpec(memory_space=pltpu.SMEM)]
        + [pl.BlockSpec(memory_space=pltpu.VMEM)] * (count + 3),
        out_specs=pl.BlockSpec(memory_space=pltpu.VMEM),
        scratch_shapes=[
            pltpu.VMEM((2, count * span, 256), BF16),
            pltpu.VMEM((2, span, 256), F32),
        ],
        compiler_params=pltpu.CompilerParams(vmem_limit_bytes=VMEM_LIMIT),
        name="totals",
    )(halves, *p_blocks, basis, lag_t, inverse)


def merge_kernel(offsets, depth, place_ref, scale_ref, *refs):
    count = len(offsets)
    d_refs, lag_ref, out_ref, square = refs[:count], refs[count], refs[count + 1], refs[count + 2]
    mm = 128 // count
    h, step = pl.program_id(0), pl.program_id(1)
    for b in range(depth):
        for j in range(count):
            start = pl.multiple_of(place_ref[j] * mm, mm)
            square[b, pl.ds(start, mm), :] = d_refs[j][0, pl.ds(b * mm, mm), :].astype(F32)
        for i in range(2):
            a = 2 * (step * depth + b) + i
            lag = lag_ref[0, 2 * b + i].astype(F32)
            turned = square[b, :, 128 * i : 128 * (i + 1)].T
            out_ref[0, 2 * b + i] = scale_ref[0, h, a] * lag + scale_ref[1, h, a] * turned


def merge(place, scales, parts, offsets, markov):
    count = len(parts)
    halves, blocks, _, _ = markov.shape
    mm = 128 // count
    depth = 4
    steps = blocks // 2 // depth
    return pl.pallas_call(
        functools.partial(merge_kernel, tuple(offsets), depth),
        out_shape=jax.ShapeDtypeStruct(markov.shape, F32),
        grid=(halves, steps),
        in_specs=[pl.BlockSpec(memory_space=pltpu.SMEM)] * 2
        + [pl.BlockSpec((1, depth * mm, 256), lambda h, s: (h, s, 0))] * count
        + [pl.BlockSpec((1, 2 * depth, 128, 128), lambda h, s: (h, s, 0, 0))],
        out_specs=pl.BlockSpec((1, 2 * depth, 128, 128), lambda h, s: (h, s, 0, 0)),
        scratch_shapes=[pltpu.VMEM((depth, 128, 256), F32)],
        compiler_params=pltpu.CompilerParams(vmem_limit_bytes=VMEM_LIMIT),
        name="merge",
    )(place, scales, *parts, markov)


def local(markov, omega):
    n_rows, n_cols = lax.axis_size("row"), lax.axis_size("col")
    r, c = lax.axis_index("row"), lax.axis_index("col")
    _, blocks, out_rows, columns = markov.shape
    rank = omega.shape[1]
    assert out_rows == 128 and columns == 128 and rank == 64
    kk, mm = rank // n_rows, columns // n_rows
    count = n_rows + 1
    pairs = blocks // 2
    rows = blocks * n_rows
    distance = [count - 1 - e for e in range(count)]
    halves = (c - jnp.arange(count - 1, -1, -1, dtype=jnp.int32) < 0).astype(jnp.int32)

    own = omega.reshape(pairs, 2, columns, rank).transpose(0, 3, 1, 2).reshape(pairs, rank, 256)
    own = lax.dynamic_slice_in_dim(own, r * kk, kk, 1)
    got = {0: own}
    d = 1
    while len(got) < count:
        got.update({k + d: shift_col(v, d) for k, v in list(got.items()) if k + d < count})
        d *= 2
    w_blocks = [got[d] for d in distance]

    lag_t = lax.dynamic_slice_in_dim(markov, r * mm, mm, 3)
    lag_t = lag_t.reshape(2, pairs, 2, out_rows, mm).transpose(0, 1, 4, 2, 3).reshape(2, pairs * mm, 256)

    partial = sketch_part(halves, markov, w_blocks, rows)
    partial = lax.all_to_all(partial, "col", 0, 0, tiled=True)
    chunk = partial.reshape(n_cols, rows // n_cols, kk, 128).astype(F32).sum(0).astype(BF16)
    spread = jnp.broadcast_to(chunk[None], (n_cols,) + chunk.shape)
    spread = lax.all_to_all(spread, "col", 0, 0, tiled=True).reshape(rows, kk, 128)
    sketches, _ = gather_row(spread)

    basis, parts = project(halves, sketches, lag_t, count)
    mine = parts[count - 1].astype(F32)
    for d in range(1, count):
        mine = mine + shift_col(parts[count - 1 - d], -d).astype(F32)
    mine = mine.astype(BF16)
    got = {0: mine}
    d = 1
    while len(got) < count:
        got.update({k + d: shift_col(v, d) for k, v in list(got.items()) if k + d < count})
        d *= 2
    p_blocks = [got[d] for d in distance]

    total_rows, total_cols = rows, blocks * n_cols
    lag_ids = (
        jnp.arange(2, dtype=jnp.int32)[:, None] * total_cols
        + c * blocks
        + jnp.arange(blocks, dtype=jnp.int32)[None, :]
    )
    counts = jnp.maximum(
        jnp.minimum(lag_ids, total_rows - 1) - jnp.maximum(0, lag_ids - total_cols + 1) + 1, 0
    )
    inverse = 1.0 / jnp.maximum(counts.astype(F32), 1.0)
    inverse = jnp.repeat(inverse, 128, axis=1).reshape(2, pairs, 1, 256)
    part = totals(halves, p_blocks, basis, lag_t, inverse)

    parts, offsets = gather_row(part)
    place = jnp.stack([r ^ o for o in offsets]).astype(jnp.int32)
    full = counts > 0
    scales = jnp.stack([jnp.where(full, 0.5 + 0.5 * SHARE, 1.0), jnp.where(full, 0.5, 0.0)]).astype(F32)
    return merge(place, scales, parts, offsets, markov)


def solution(mesh):
    in_specs = (P(None, "col", None, None), P("col", None))
    out_specs = P(None, "col", None, None)
    return jax.shard_map(local, mesh=mesh, in_specs=in_specs, out_specs=out_specs, check_vma=False)
```

```python
import functools

import jax
import jax.numpy as jnp
from jax import lax
from jax.experimental import pallas as pl
from jax.experimental.pallas import tpu as pltpu
from jax.sharding import PartitionSpec as P

NS_STEPS = 8
norm_floor = 1e-06
SHARE = 0.375
F32 = jnp.float32
BF16 = jnp.bfloat16
HIGHEST = lax.Precision.HIGHEST
VMEM_LIMIT = 56 * 1024 * 1024

NT = (((1,), (1,)), ((), ()))
NN = (((1,), (0,)), ((), ()))


def matmul(left, right, dims=NN):
    return lax.dot_general(left, right, dims, preferred_element_type=F32)


def shift_col(x, distance):
    n = lax.axis_size("col")
    return lax.ppermute(x, "col", [(i, (i + distance) % n) for i in range(n)])


def swap_row(x, bit):
    n = lax.axis_size("row")
    return lax.ppermute(x, "row", [(i, i ^ bit) for i in range(n)])


def gather_row(x):
    pieces, offsets = [x], [0]
    bit = lax.axis_size("row") // 2
    while bit:
        pieces = pieces + [swap_row(p, bit) for p in pieces]
        offsets = offsets + [o ^ bit for o in offsets]
        bit //= 2
    return pieces, offsets


def half_of(ids_ref, count, e):
    return jnp.where(ids_ref[1] < count - 1 - e, 1, 0)


def lag_count(lag, total_rows, total_cols):
    low = jnp.maximum(0, lag - total_cols + 1)
    return jnp.maximum(jnp.minimum(lag, total_rows - 1) - low + 1, 0)


def sketch_kernel(count, ids_ref, lag_ref, *refs):
    w_refs = refs[:count]
    out_ref, lags, padded, sems = refs[count:]
    blocks = lag_ref.shape[1]
    pairs, kk, _ = w_refs[0].shape
    copies = [
        pltpu.make_async_copy(lag_ref.at[h], lags.at[h, pl.ds(1, blocks)], sems.at[h]) for h in range(2)
    ]
    for copy in copies:
        copy.start()
    zero = jnp.zeros(lags.shape[2:], BF16)
    for h in range(2):
        lags[h, 0] = zero
        lags[h, blocks + 1] = zero
        lags[h, blocks + 2] = zero
    for e in range(count):
        padded[e, pl.ds(0, pairs)] = jnp.zeros((pairs, kk, 256), BF16)
        padded[e, pl.ds(pairs, pairs)] = w_refs[e][...]
        padded[e, pl.ds(2 * pairs, pairs + 1)] = jnp.zeros((pairs + 1, kk, 256), BF16)
    for copy in copies:
        copy.wait()

    size = pairs + 1

    def tile_of(h, t):
        before, here, after = lags[h, 2 * t], lags[h, 2 * t + 1], lags[h, 2 * t + 2]
        return jnp.concatenate(
            [jnp.concatenate([before, here], 1), jnp.concatenate([here, after], 1)], 0
        )

    def store(f, total):
        total = total.reshape(size, kk, 256).astype(BF16)
        for x in range(pairs):
            out_ref[f * 2 * pairs + 2 * x] = total[x, :, :128]
            out_ref[f * 2 * pairs + 2 * x + 1] = total[x + 1, :, 128:]

    def step(f, carry):
        low, high = half_of(ids_ref, count, f), half_of(ids_ref, count, f + 1)

        @pl.when(low == high)
        def _():
            total = jnp.zeros((size * kk, 256), F32)
            for t in range(size):
                rows = [padded[f, pl.ds(pairs + t, pairs - t)]] if t < pairs else []
                rows.append(padded[f + 1, pl.ds(pairs, t + 1)])
                rows = jnp.concatenate(rows, 0) if len(rows) > 1 else rows[0]
                total += matmul(rows.reshape(size * kk, 256), tile_of(low, t), NT)
            store(f, total)

        @pl.when(low != high)
        def _():
            total = jnp.zeros((size * kk, 256), F32)
            for side, h in enumerate((low, high)):
                for t in range(size):
                    first = t if side else pairs + t
                    rows = padded[f + side, pl.ds(first, size)].reshape(size * kk, 256)
                    total += matmul(rows, tile_of(h, t), NT)
            store(f, total)

        return carry

    lax.fori_loop(0, count - 1, step, 0)


def sketch_part(ids, markov, w_blocks, rows):
    count = len(w_blocks)
    blocks = markov.shape[1]
    pairs, kk, _ = w_blocks[0].shape
    return pl.pallas_call(
        functools.partial(sketch_kernel, count),
        out_shape=jax.ShapeDtypeStruct((rows, kk, 128), BF16),
        in_specs=[pl.BlockSpec(memory_space=pltpu.SMEM), pl.BlockSpec(memory_space=pl.ANY)]
        + [pl.BlockSpec(memory_space=pltpu.VMEM)] * count,
        out_specs=pl.BlockSpec(memory_space=pltpu.VMEM),
        scratch_shapes=[
            pltpu.VMEM((2, blocks + 3, 128, 128), BF16),
            pltpu.VMEM((count, 3 * pairs + 1, kk, 256), BF16),
            pltpu.SemaphoreType.DMA((2,)),
        ],
        compiler_params=pltpu.CompilerParams(vmem_limit_bytes=VMEM_LIMIT),
        name="sketch",
    )(ids, markov, *w_blocks)


def split(x):
    high = x.astype(BF16)
    return high, (x - high.astype(F32)).astype(BF16)


def full_dot(left, right):
    return jnp.dot(left, right, precision=HIGHEST, preferred_element_type=F32)


def newton_schulz(gram):
    size = gram.shape[0]
    row = lax.broadcasted_iota(jnp.int32, (size, size), 0)
    col = lax.broadcasted_iota(jnp.int32, (size, size), 1)
    eye = jnp.where(row == col, 1.0, 0.0)
    scale = 1.0 / jnp.sqrt(jnp.sum(gram * eye, keepdims=True) + norm_floor)
    inner = gram * (scale * scale)
    coeffs = eye * scale
    for sweep in range(NS_STEPS):
        update = 1.5 * eye - 0.5 * inner
        coeffs = full_dot(coeffs, update)
        if sweep + 1 < NS_STEPS:
            inner = full_dot(full_dot(inner, update), update)
    return coeffs


def basis_tile(basis_ref, g, rank):
    low = g * 256 if isinstance(g, int) else pl.multiple_of(g * 256, 256)
    return jnp.concatenate(
        [basis_ref[pl.ds(low + rank, 256), :], basis_ref[pl.ds(low, 256), :]], 1
    )


def project_kernel(count, pieces, ids_ref, *refs):
    s_refs = refs[:pieces]
    lt_ref, basis_ref = refs[pieces : pieces + 2]
    out_refs = refs[pieces + 2 : pieces + 2 + count]
    sketch, gram4, padded = refs[pieces + 2 + count :]
    rows, kk, _ = s_refs[0].shape
    rank = kk * pieces
    group = 256 // rank
    pairs, mm, _ = out_refs[0].shape
    groups = rows // group
    batch = 8

    gram4[...] = jnp.zeros_like(gram4)
    for h in range(2):
        padded[h, pl.ds(0, pairs - 1)] = jnp.zeros((pairs - 1, mm, 256), BF16)
        padded[h, pl.ds(pairs - 1, pairs)] = lt_ref[h].reshape(pairs, mm, 256)
        padded[h, pl.ds(2 * pairs - 1, pairs)] = jnp.zeros((pairs, mm, 256), BF16)

    def load(s, carry):
        blocks = []
        for k in range(batch):
            g = s * batch + k
            block = jnp.concatenate(
                [s_refs[j][group * g + i] for i in range(group) for j in range(pieces)], 0
            )
            sketch[pl.ds(pl.multiple_of(g * 256, 256), 256), :] = block
            blocks.append(block)
        wide = jnp.concatenate(blocks, 1)
        gram4[...] += matmul(wide, wide, NT)
        return carry

    lax.fori_loop(0, groups // batch, load, 0)
    gram = sum(
        gram4[rank * i : rank * (i + 1), rank * i : rank * (i + 1)] for i in range(group)
    )
    coeffs = newton_schulz(gram)
    wide = jnp.concatenate([coeffs] * group, 1)
    wide = jnp.concatenate([wide] * group, 0)
    row = lax.broadcasted_iota(jnp.int32, (256, 256), 0) // rank
    col = lax.broadcasted_iota(jnp.int32, (256, 256), 1) // rank
    wide = jnp.where(row == col, wide, 0.0)
    both = jnp.concatenate(split(wide), 1)

    basis_ref[pl.ds(0, 2 * rank), :] = jnp.zeros((2 * rank, 128), BF16)
    basis_ref[pl.ds((rows + 2) * rank, 3 * rank), :] = jnp.zeros((3 * rank, 128), BF16)

    def rotate(s, carry):
        for k in range(batch // 2):
            first = pl.multiple_of((s * batch + 2 * k) * 256, 256)
            block = jnp.concatenate(
                [sketch[pl.ds(first, 256), :], sketch[pl.ds(first + 256, 256), :]], 1
            )
            value = matmul(both, jnp.concatenate([block, block], 0)).astype(BF16)
            basis_ref[pl.ds(first + 2 * rank, 256), :] = value[:, :128]
            basis_ref[pl.ds(first + 2 * rank + 256, 256), :] = value[:, 128:]
        return carry

    lax.fori_loop(0, groups // batch, rotate, 0)
    half = pairs // 2

    for e in range(count):
        h = half_of(ids_ref, count, e)
        total = jnp.zeros(((pairs + 1) * mm, 256), F32)
        for k in range(pairs):
            g = half * (e - 1) + k
            if 0 <= g <= groups:
                rows_k = padded[h, pl.ds(2 * pairs - 2 - 2 * k, pairs + 1)].reshape((pairs + 1) * mm, 256)
                total += matmul(rows_k, basis_tile(basis_ref, g, rank), NT)
        total = total.reshape(pairs + 1, mm, 256)
        out_refs[e][...] = (total[1:, :, :128] + total[:-1, :, 128:]).astype(BF16)


def project(ids, sketches, lag_t, count):
    pieces = len(sketches)
    rows, kk, _ = sketches[0].shape
    rank = kk * pieces
    mm = 128 // pieces
    pairs = lag_t.shape[1] // mm
    return pl.pallas_call(
        functools.partial(project_kernel, count, pieces),
        out_shape=[
            jax.ShapeDtypeStruct(((rows + 5) * rank, 128), BF16),
        ]
        + [jax.ShapeDtypeStruct((pairs, mm, 128), BF16)] * count,
        in_specs=[pl.BlockSpec(memory_space=pltpu.SMEM)]
        + [pl.BlockSpec(memory_space=pltpu.VMEM)] * (pieces + 1),
        out_specs=[pl.BlockSpec(memory_space=pltpu.VMEM)] * (count + 1),
        scratch_shapes=[
            pltpu.VMEM((rows * rank, 128), BF16),
            pltpu.VMEM((256, 256), F32),
            pltpu.VMEM((2, 3 * pairs - 1, mm, 256), BF16),
        ],
        compiler_params=pltpu.CompilerParams(vmem_limit_bytes=VMEM_LIMIT),
        name="project",
    )(ids, *sketches, lag_t)


def totals_kernel(count, total_cols, ids_ref, *refs):
    p_refs = refs[:count]
    basis_ref, lt_ref, out_ref, wide, acc = refs[count:]
    pairs, mm, _ = p_refs[0].shape
    span = pairs * mm
    half = pairs // 2
    for h in range(2):
        wide[h, pl.ds(count * span - mm, mm), 128:] = jnp.zeros((mm, 128), BF16)
    for e in range(count):
        block = p_refs[e][...].reshape(span, 128)
        zero = jnp.zeros_like(block)
        for h in range(2):
            kept = jnp.where(half_of(ids_ref, count, e) == h, block, zero)
            wide[h, pl.ds(e * span, span), :128] = kept
            if e == 0:
                wide[h, pl.ds(0, span - mm), 128:] = kept[mm:]
            else:
                wide[h, pl.ds(e * span - mm, span), 128:] = kept
    acc[...] = jnp.zeros_like(acc)

    def chain(h, first, size):
        total = jnp.zeros((span, 256), F32)
        for k in range(size):
            start = pl.multiple_of((first + k) * 2 * mm, 32)
            total += matmul(wide[h, pl.ds(start, span), :], basis_tile(basis_ref, first + k, 64))
        acc[h] += total

    def step(e, carry):
        for h in range(2):
            here, after = half_of(ids_ref, count, e) == h, half_of(ids_ref, count, e + 1) == h

            @pl.when(jnp.logical_or(here, after))
            def _():
                chain(h, e * half, half)

        return carry

    lax.fori_loop(0, count - 1, step, 0)
    chain(0, (count - 1) * half, 1)
    blocks = 2 * pairs
    b = lax.broadcasted_iota(jnp.int32, (pairs, 1, 256), 0)
    lane = lax.broadcasted_iota(jnp.int32, (pairs, 1, 256), 2)
    for h in range(2):
        lag = h * total_cols + ids_ref[1] * blocks + 2 * b + lane // 128
        counts = lag_count(lag, blocks * (count - 1), total_cols)
        scaled = acc[h].reshape(pairs, mm, 256) * (1.0 / jnp.maximum(counts.astype(F32), 1.0))
        out_ref[h] = (scaled.reshape(span, 256) - SHARE * lt_ref[h].astype(F32)).astype(BF16)


def totals(ids, p_blocks, basis, lag_t, total_cols):
    count = len(p_blocks)
    pairs, mm, _ = p_blocks[0].shape
    span = pairs * mm
    return pl.pallas_call(
        functools.partial(totals_kernel, count, total_cols),
        out_shape=jax.ShapeDtypeStruct((2, span, 256), BF16),
        in_specs=[pl.BlockSpec(memory_space=pltpu.SMEM)]
        + [pl.BlockSpec(memory_space=pltpu.VMEM)] * (count + 2),
        out_specs=pl.BlockSpec(memory_space=pltpu.VMEM),
        scratch_shapes=[
            pltpu.VMEM((2, count * span, 256), BF16),
            pltpu.VMEM((2, span, 256), F32),
        ],
        compiler_params=pltpu.CompilerParams(vmem_limit_bytes=VMEM_LIMIT),
        name="totals",
    )(ids, *p_blocks, basis, lag_t)


def merge_kernel(offsets, depth, total_rows, total_cols, ids_ref, *refs):
    count = len(offsets)
    d_refs, lag_ref, out_ref, square = refs[:count], refs[count], refs[count + 1], refs[count + 2]
    mm = 128 // count
    h, step = pl.program_id(0), pl.program_id(1)
    blocks = 2 * depth * pl.num_programs(1)
    row = lax.broadcasted_iota(jnp.int32, (128, 128), 0)
    col = lax.broadcasted_iota(jnp.int32, (128, 128), 1)
    eye = jnp.where(row == col, 1.0, 0.0).astype(BF16)
    for j in range(count):
        start = pl.multiple_of((ids_ref[0] ^ offsets[j]) * mm, mm)
        for b in range(depth):
            square[b, pl.ds(start, mm), :] = d_refs[j][0, pl.ds(b * mm, mm), :]
    for b in range(depth):
        for i in range(2):
            a = 2 * (step * depth + b) + i
            full = lag_count(h * total_cols + ids_ref[1] * blocks + a, total_rows, total_cols) > 0
            keep = jnp.where(full, 0.5 + 0.5 * SHARE, 1.0)
            gain = jnp.where(full, 0.5, 0.0)
            turned = matmul(eye, square[b, :, 128 * i : 128 * (i + 1)], NT)
            out_ref[0, 2 * b + i] = keep * lag_ref[0, 2 * b + i].astype(F32) + gain * turned


def merge(ids, parts, offsets, markov, total_rows, total_cols):
    count = len(parts)
    halves, blocks, _, _ = markov.shape
    mm = 128 // count
    depth = blocks // 2
    steps = blocks // 2 // depth
    return pl.pallas_call(
        functools.partial(merge_kernel, tuple(offsets), depth, total_rows, total_cols),
        out_shape=jax.ShapeDtypeStruct(markov.shape, F32),
        grid=(halves, steps),
        in_specs=[pl.BlockSpec(memory_space=pltpu.SMEM)]
        + [pl.BlockSpec((1, depth * mm, 256), lambda h, s: (h, s, 0))] * count
        + [pl.BlockSpec((1, 2 * depth, 128, 128), lambda h, s: (h, s, 0, 0))],
        out_specs=pl.BlockSpec((1, 2 * depth, 128, 128), lambda h, s: (h, s, 0, 0)),
        scratch_shapes=[pltpu.VMEM((depth, 128, 256), BF16)],
        compiler_params=pltpu.CompilerParams(vmem_limit_bytes=VMEM_LIMIT),
        name="merge",
    )(ids, *parts, markov)


def spread_rounds(count):
    rounds = [[(d, [0]) for d in (1, 2) if d < count]]
    have, shift = 3, 2
    while have < count:
        last = min(have + shift, count)
        rounds.append([(shift, list(range(have - shift, last - shift)))])
        have, shift = last, shift * 2
    return rounds


def spread_blocks(own, count, extra=None):
    got = {0: own}
    for step in spread_rounds(count):
        got.update({k + d: shift_col(got[k], d) for d, ks in step for k in ks})
        if extra is not None:
            got, extra = lax.optimization_barrier((got, extra))
    return got, extra


def collect_blocks(parts, count):
    total = {d: parts[d].astype(F32) for d in range(count)}
    for step in reversed(spread_rounds(count)):
        moved = [(k, shift_col(total[k + d].astype(BF16), -d)) for d, ks in step for k in ks]
        for k, block in moved:
            total[k] = total[k] + block.astype(F32)
    return total[0].astype(BF16)


def local(markov, omega):
    n_rows, n_cols = lax.axis_size("row"), lax.axis_size("col")
    r, c = lax.axis_index("row"), lax.axis_index("col")
    _, blocks, out_rows, columns = markov.shape
    rank = omega.shape[1]
    assert out_rows == 128 and columns == 128 and rank == 64
    kk, mm = rank // n_rows, columns // n_rows
    count = n_rows + 1
    pairs = blocks // 2
    rows = blocks * n_rows
    total_cols = blocks * n_cols
    distance = [count - 1 - e for e in range(count)]
    ids = jnp.stack([r, c]).astype(jnp.int32)

    own = omega.reshape(pairs, 2, columns, rank).transpose(0, 3, 1, 2).reshape(pairs, rank, 256)
    own = lax.dynamic_slice_in_dim(own, r * kk, kk, 1)
    lag_t = lax.dynamic_slice_in_dim(markov, r * mm, mm, 3)
    lag_t = lag_t.reshape(2, pairs, 2, out_rows, mm).transpose(0, 1, 4, 2, 3).reshape(2, pairs * mm, 256)
    got, lag_t = spread_blocks(own, count, lag_t)
    w_blocks = [got[d] for d in distance]

    partial = sketch_part(ids, markov, w_blocks, rows)
    partial = lax.all_to_all(partial, "col", 0, 0, tiled=True)
    chunk = partial.reshape(n_cols, rows // n_cols, kk, 128).astype(F32).sum(0).astype(BF16)
    spread = jnp.broadcast_to(chunk[None], (n_cols,) + chunk.shape)
    spread = lax.all_to_all(spread, "col", 0, 0, tiled=True).reshape(rows, kk, 128)
    sketches, _ = gather_row(spread)

    basis, *parts = project(ids, sketches, lag_t, count)
    mine = collect_blocks({d: parts[count - 1 - d] for d in range(count)}, count)
    got, _ = spread_blocks(mine, count)
    p_blocks = [got[d] for d in distance]

    part = totals(ids, p_blocks, basis, lag_t, total_cols)
    parts, offsets = gather_row(part)
    return merge(ids, parts, offsets, markov, rows, total_cols)


def solution(mesh):
    in_specs = (P(None, "col", None, None), P("col", None))
    out_specs = P(None, "col", None, None)
    return jax.shard_map(local, mesh=mesh, in_specs=in_specs, out_specs=out_specs, check_vma=False)
```

```python
import functools

import jax
import jax.numpy as jnp
from jax import lax
from jax.experimental import pallas as pl
from jax.experimental.pallas import tpu as pltpu
from jax.sharding import PartitionSpec as P


NS_STEPS = 8
norm_floor = 1e-06
SHARE = 0.375
F32 = jnp.float32
BF16 = jnp.bfloat16
HIGHEST = lax.Precision.HIGHEST
VMEM_LIMIT = 56 * 1024 * 1024

NT = (((1,), (1,)), ((), ()))
NN = (((1,), (0,)), ((), ()))


def matmul(left, right, dims=NN):
    return lax.dot_general(left, right, dims, preferred_element_type=F32)


def shift_col(x, distance):
    n = lax.axis_size("col")
    return lax.ppermute(x, "col", [(i, (i + distance) % n) for i in range(n)])


def swap(axis, x, bit):
    n = lax.axis_size(axis)
    return lax.ppermute(x, axis, [(i, i ^ bit) for i in range(n)])


def gather_row(x):
    pieces, offsets = [x], [0]
    bit = lax.axis_size("row") // 2
    while bit:
        pieces = pieces + [swap("row", p, bit) for p in pieces]
        offsets = offsets + [o ^ bit for o in offsets]
        bit //= 2
    return pieces, offsets


def half_of(ids_ref, count, e):
    return jnp.where(ids_ref[1] < count - 1 - e, 1, 0)


def lag_count(lag, total_rows, total_cols):
    low = jnp.maximum(0, lag - total_cols + 1)
    return jnp.maximum(jnp.minimum(lag, total_rows - 1) - low + 1, 0)


def sketch_kernel(count, first, last, ids_ref, lag_ref, *refs):
    w_refs = refs[: last - first + 1]
    out_ref, lags, padded, sems = refs[-4:]
    blocks = lag_ref.shape[1]
    pairs, kk, _ = w_refs[0].shape
    copies = [
        pltpu.make_async_copy(lag_ref.at[h], lags.at[h, pl.ds(1, blocks)], sems.at[h]) for h in range(2)
    ]
    for copy in copies:
        copy.start()
    zero = jnp.zeros(lags.shape[2:], BF16)
    for h in range(2):
        lags[h, 0] = zero
        lags[h, blocks + 1] = zero
        lags[h, blocks + 2] = zero
    for e in range(last - first + 1):
        padded[e, pl.ds(0, pairs)] = jnp.zeros((pairs, kk, 256), BF16)
        padded[e, pl.ds(pairs, pairs)] = w_refs[e][...]
        padded[e, pl.ds(2 * pairs, pairs + 1)] = jnp.zeros((pairs + 1, kk, 256), BF16)
    for copy in copies:
        copy.wait()

    size = pairs + 1

    def tile_of(h, t):
        before, here, after = lags[h, 2 * t], lags[h, 2 * t + 1], lags[h, 2 * t + 2]
        return jnp.concatenate(
            [jnp.concatenate([before, here], 1), jnp.concatenate([here, after], 1)], 0
        )

    def store(f, total):
        total = total.reshape(size, kk, 256).astype(BF16)
        for x in range(pairs):
            out_ref[f * 2 * pairs + 2 * x] = total[x, :, :128]
            out_ref[f * 2 * pairs + 2 * x + 1] = total[x + 1, :, 128:]

    def step(f, carry):
        low, high = half_of(ids_ref, count, first + f), half_of(ids_ref, count, first + f + 1)

        @pl.when(low == high)
        def _():
            total = jnp.zeros((size * kk, 256), F32)
            for t in range(size):
                rows = [padded[f, pl.ds(pairs + t, pairs - t)]] if t < pairs else []
                rows.append(padded[f + 1, pl.ds(pairs, t + 1)])
                rows = jnp.concatenate(rows, 0) if len(rows) > 1 else rows[0]
                total += matmul(rows.reshape(size * kk, 256), tile_of(low, t), NT)
            store(f, total)

        @pl.when(low != high)
        def _():
            total = jnp.zeros((size * kk, 256), F32)
            for side, h in enumerate((low, high)):
                for t in range(size):
                    offset = t if side else pairs + t
                    rows = padded[f + side, pl.ds(offset, size)].reshape(size * kk, 256)
                    total += matmul(rows, tile_of(h, t), NT)
            store(f, total)

        return carry

    lax.fori_loop(0, last - first, step, 0)


def sketch_part(ids, markov, w_blocks, first, last, rows, before=None):
    count = rows // markov.shape[1] + 1
    blocks = markov.shape[1]
    pairs, kk, _ = w_blocks[first].shape
    used = [w_blocks[e] for e in range(first, last + 1)]
    height = (last - first) * blocks
    place = first // (last - first)
    return pl.pallas_call(
        functools.partial(sketch_kernel, count, first, last),
        out_shape=jax.ShapeDtypeStruct((rows, kk, 128), BF16),
        grid=(1,),
        in_specs=[pl.BlockSpec(memory_space=pltpu.SMEM), pl.BlockSpec(memory_space=pl.ANY)]
        + [pl.BlockSpec(memory_space=pltpu.VMEM)] * len(used)
        + ([] if before is None else [pl.BlockSpec(memory_space=pl.ANY)]),
        out_specs=pl.BlockSpec((height, kk, 128), lambda i: (place, 0, 0)),
        input_output_aliases={} if before is None else {2 + len(used): 0},
        scratch_shapes=[
            pltpu.VMEM((2, blocks + 3, 128, 128), BF16),
            pltpu.VMEM((len(used), 3 * pairs + 1, kk, 256), BF16),
            pltpu.SemaphoreType.DMA((2,)),
        ],
        compiler_params=pltpu.CompilerParams(vmem_limit_bytes=VMEM_LIMIT),
        name="sketch",
    )(ids, markov, *used, *([] if before is None else [before]))


def split(x):
    high = x.astype(BF16)
    return high, (x - high.astype(F32)).astype(BF16)


def full_dot(left, right):
    return jnp.dot(left, right, precision=HIGHEST, preferred_element_type=F32)


def newton_schulz(gram):
    size = gram.shape[0]
    row = lax.broadcasted_iota(jnp.int32, (size, size), 0)
    col = lax.broadcasted_iota(jnp.int32, (size, size), 1)
    eye = jnp.where(row == col, 1.0, 0.0)
    scale = 1.0 / jnp.sqrt(jnp.sum(gram * eye, keepdims=True) + norm_floor)
    inner = gram * (scale * scale)
    coeffs = eye * scale
    for sweep in range(NS_STEPS):
        update = 1.5 * eye - 0.5 * inner
        coeffs = full_dot(coeffs, update)
        if sweep + 1 < NS_STEPS:
            inner = full_dot(full_dot(inner, update), update)
    return coeffs


def basis_tile(basis_ref, g, rank):
    low = g * 256 if isinstance(g, int) else pl.multiple_of(g * 256, 256)
    return jnp.concatenate(
        [basis_ref[pl.ds(low + rank, 256), :], basis_ref[pl.ds(low, 256), :]], 1
    )


def pad_lags(lt_ref, padded):
    pairs = (padded.shape[1] + 1) // 3
    mm = padded.shape[2]
    for h in range(2):
        padded[h, pl.ds(0, pairs - 1)] = jnp.zeros((pairs - 1, mm, 256), BF16)
        padded[h, pl.ds(pairs - 1, pairs)] = lt_ref[h].reshape(pairs, mm, 256)
        padded[h, pl.ds(2 * pairs - 1, pairs)] = jnp.zeros((pairs, mm, 256), BF16)


def project_block(count, rank, e, ids_ref, basis_ref, padded):
    pairs = (padded.shape[1] + 1) // 3
    mm = padded.shape[2]
    groups = (basis_ref.shape[0] // rank - 5) // (256 // rank)
    h = half_of(ids_ref, count, e)
    total = jnp.zeros(((pairs + 1) * mm, 256), F32)
    for k in range(pairs):
        g = pairs // 2 * (e - 1) + k
        if 0 <= g <= groups:
            rows_k = padded[h, pl.ds(2 * pairs - 2 - 2 * k, pairs + 1)].reshape((pairs + 1) * mm, 256)
            total += matmul(rows_k, basis_tile(basis_ref, g, rank), NT)
    total = total.reshape(pairs + 1, mm, 256)
    return (total[1:, :, :128] + total[:-1, :, 128:]).astype(BF16)


def project_rest_kernel(count, rank, ids_ref, basis_ref, lt_ref, middle_ref, own_ref, padded):
    pad_lags(lt_ref, padded)
    late = middle_ref.shape[0]
    for e in range(late, count - 1):
        middle_ref[e - late] = project_block(count, rank, e, ids_ref, basis_ref, padded)
    own_ref[...] = project_block(count, rank, count - 1, ids_ref, basis_ref, padded)


def project_kernel(count, pieces, ids_ref, *refs):
    s_refs = refs[:pieces]
    lt_ref, basis_ref, far_ref, sketch, gram4, padded = refs[pieces:]
    steps, height, kk, _ = s_refs[0].shape
    rows = 2 * steps * height
    sides = pieces // 2
    rank = kk * sides
    group = 256 // rank
    groups = rows // group
    batch = 8

    gram4[...] = jnp.zeros_like(gram4)
    pad_lags(lt_ref, padded)
    for j in range(steps):
        blocks = []
        for side in range(2):
            chunk = lax.rem((ids_ref[1] ^ side) - 2 * j + 2 * steps, 2 * steps)
            for i in range(height // group):
                block = jnp.concatenate(
                    [
                        s_refs[side * sides + q][j, group * i + x]
                        for x in range(group)
                        for q in range(sides)
                    ],
                    0,
                )
                start = pl.multiple_of(chunk * (height * rank) + 256 * i, 256)
                sketch[pl.ds(start, 256), :] = block
                blocks.append(block)
        wide = jnp.concatenate(blocks, 1)
        gram4[...] += matmul(wide, wide, NT)
    gram = sum(
        gram4[rank * i : rank * (i + 1), rank * i : rank * (i + 1)] for i in range(group)
    )
    coeffs = newton_schulz(gram)
    wide = jnp.concatenate([coeffs] * group, 1)
    wide = jnp.concatenate([wide] * group, 0)
    row = lax.broadcasted_iota(jnp.int32, (256, 256), 0) // rank
    col = lax.broadcasted_iota(jnp.int32, (256, 256), 1) // rank
    wide = jnp.where(row == col, wide, 0.0)
    both = jnp.concatenate(split(wide), 1)

    basis_ref[pl.ds(0, 2 * rank), :] = jnp.zeros((2 * rank, 128), BF16)
    basis_ref[pl.ds((rows + 2) * rank, 3 * rank), :] = jnp.zeros((3 * rank, 128), BF16)

    def rotate(s, carry):
        for k in range(batch // 2):
            first = pl.multiple_of((s * batch + 2 * k) * 256, 256)
            block = jnp.concatenate(
                [sketch[pl.ds(first, 256), :], sketch[pl.ds(first + 256, 256), :]], 1
            )
            value = matmul(both, jnp.concatenate([block, block], 0)).astype(BF16)
            basis_ref[pl.ds(first + 2 * rank, 256), :] = value[:, :128]
            basis_ref[pl.ds(first + 2 * rank + 256, 256), :] = value[:, 128:]
        return carry

    lax.fori_loop(0, groups // batch, rotate, 0)
    for e in range(far_ref.shape[0]):
        far_ref[e] = project_block(count, rank, e, ids_ref, basis_ref, padded)


def project(ids, sketches, lag_t, count):
    pieces = len(sketches)
    steps, height, kk, _ = sketches[0].shape
    rows = 2 * steps * height
    rank = kk * pieces // 2
    mm = 128 * 2 // pieces
    pairs = lag_t.shape[1] // mm
    return pl.pallas_call(
        functools.partial(project_kernel, count, pieces),
        out_shape=[
            jax.ShapeDtypeStruct(((rows + 5) * rank, 128), BF16),
            jax.ShapeDtypeStruct((count // 2, pairs, mm, 128), BF16),
        ],
        in_specs=[pl.BlockSpec(memory_space=pltpu.SMEM)]
        + [pl.BlockSpec(memory_space=pltpu.VMEM)] * (pieces + 1),
        out_specs=[pl.BlockSpec(memory_space=pltpu.VMEM)] * 2,
        scratch_shapes=[
            pltpu.VMEM((rows * rank, 128), BF16),
            pltpu.VMEM((256, 256), F32),
            pltpu.VMEM((2, 3 * pairs - 1, mm, 256), BF16),
        ],
        compiler_params=pltpu.CompilerParams(vmem_limit_bytes=VMEM_LIMIT),
        name="project",
    )(ids, *sketches, lag_t)


def project_rest(ids, basis, lag_t, count, rank):
    mm = 128 // (count - 1)
    pairs = lag_t.shape[1] // mm
    return pl.pallas_call(
        functools.partial(project_rest_kernel, count, rank),
        out_shape=[
            jax.ShapeDtypeStruct((count // 2, pairs, mm, 128), BF16),
            jax.ShapeDtypeStruct((pairs, mm, 128), BF16),
        ],
        in_specs=[pl.BlockSpec(memory_space=pltpu.SMEM)] + [pl.BlockSpec(memory_space=pltpu.VMEM)] * 2,
        out_specs=[pl.BlockSpec(memory_space=pltpu.VMEM)] * 2,
        scratch_shapes=[pltpu.VMEM((2, 3 * pairs - 1, mm, 256), BF16)],
        compiler_params=pltpu.CompilerParams(vmem_limit_bytes=VMEM_LIMIT),
        name="project_rest",
    )(ids, basis, lag_t)


def totals_kernel(count, halves, first, last, ids_ref, *refs):
    number = last - first + 1
    p_refs = refs[:number]
    final = first == 0
    if final:
        basis_ref, sums_ref, lt_ref, out_ref, wide, acc = refs[number:]
    else:
        basis_ref, acc, wide = refs[number:]
    pairs, mm, _ = p_refs[0].shape
    span = pairs * mm
    half = pairs // 2
    for x, h in enumerate(halves):
        wide[x, pl.ds(number * span - mm, mm), 128:] = jnp.zeros((mm, 128), BF16)
        acc[x] = sums_ref[h] if final else jnp.zeros((span, 256), F32)
    for e in range(number):
        block = p_refs[e][...].reshape(span, 128)
        zero = jnp.zeros_like(block)
        for x, h in enumerate(halves):
            kept = jnp.where(half_of(ids_ref, count, first + e) == h, block, zero)
            wide[x, pl.ds(e * span, span), :128] = kept
            if e == 0:
                wide[x, pl.ds(0, span - mm), 128:] = kept[mm:]
            else:
                wide[x, pl.ds(e * span - mm, span), 128:] = kept

    def chain(x, e, size):
        total = jnp.zeros((span, 256), F32)
        for k in range(size):
            start = pl.multiple_of((e * half + k) * 2 * mm, 32)
            tile = basis_tile(basis_ref, (first + e) * half + k, 64)
            total += matmul(wide[x, pl.ds(start, span), :], tile)
        acc[x] += total

    def step(e, carry):
        here, after = half_of(ids_ref, count, first + e), half_of(ids_ref, count, first + e + 1)
        for x, h in enumerate(halves):

            @pl.when(jnp.logical_or(here == h, after == h))
            def _():
                chain(x, e, half)

        return carry

    lax.fori_loop(0, last - first, step, 0)
    if not final:
        chain(0, last - first, 1)
        return
    blocks = 2 * pairs
    total_cols = blocks * lax.axis_size("col")
    b = lax.broadcasted_iota(jnp.int32, (pairs, 1, 256), 0)
    lane = lax.broadcasted_iota(jnp.int32, (pairs, 1, 256), 2)
    for h in halves:
        lag = h * total_cols + ids_ref[1] * blocks + 2 * b + lane // 128
        counts = lag_count(lag, blocks * (count - 1), total_cols)
        scaled = acc[h].reshape(pairs, mm, 256) * (1.0 / jnp.maximum(counts.astype(F32), 1.0))
        out_ref[h] = (scaled.reshape(span, 256) - SHARE * lt_ref[h].astype(F32)).astype(BF16)


def totals_near(ids, p_blocks, basis):
    count = len(p_blocks)
    first, last = count // 2, count - 1
    pairs, mm, _ = p_blocks[last].shape
    span = pairs * mm
    return pl.pallas_call(
        functools.partial(totals_kernel, count, (0, 1), first, last),
        out_shape=jax.ShapeDtypeStruct((2, span, 256), F32),
        in_specs=[pl.BlockSpec(memory_space=pltpu.SMEM)]
        + [pl.BlockSpec(memory_space=pltpu.VMEM)] * (last - first + 2),
        out_specs=pl.BlockSpec(memory_space=pltpu.VMEM),
        scratch_shapes=[pltpu.VMEM((2, (last - first + 1) * span, 256), BF16)],
        compiler_params=pltpu.CompilerParams(vmem_limit_bytes=VMEM_LIMIT),
        name="totals_near",
    )(ids, *p_blocks[first:], basis)


def totals_far(ids, p_blocks, basis, sums, lag_t):
    count = len(p_blocks)
    first, last = 0, count // 2
    pairs, mm, _ = p_blocks[first].shape
    span = pairs * mm
    return pl.pallas_call(
        functools.partial(totals_kernel, count, (0, 1), first, last),
        out_shape=jax.ShapeDtypeStruct((2, span, 256), BF16),
        in_specs=[pl.BlockSpec(memory_space=pltpu.SMEM)]
        + [pl.BlockSpec(memory_space=pltpu.VMEM)] * (last - first + 4),
        out_specs=pl.BlockSpec(memory_space=pltpu.VMEM),
        scratch_shapes=[
            pltpu.VMEM((2, (last - first + 1) * span, 256), BF16),
            pltpu.VMEM((2, span, 256), F32),
        ],
        compiler_params=pltpu.CompilerParams(vmem_limit_bytes=VMEM_LIMIT),
        name="totals_far",
    )(ids, *p_blocks[first : last + 1], basis, sums, lag_t)


def merge_kernel(offsets, total_rows, total_cols, ids_ref, *refs):
    count = len(offsets)
    d_refs, lag_ref, out_ref, square = refs[:count], refs[count], refs[count + 1], refs[count + 2]
    mm = 128 // count
    depth = square.shape[0]
    blocks = 2 * depth
    h = pl.program_id(0)
    row = lax.broadcasted_iota(jnp.int32, (128, 128), 0)
    col = lax.broadcasted_iota(jnp.int32, (128, 128), 1)
    eye = jnp.where(row == col, 1.0, 0.0).astype(BF16)
    for j in range(count):
        start = pl.multiple_of((ids_ref[0] ^ offsets[j]) * mm, mm)
        for b in range(depth):
            square[b, pl.ds(start, mm), :] = d_refs[j][0, pl.ds(b * mm, mm), :]
    for b in range(depth):
        for i in range(2):
            a = 2 * b + i
            full = lag_count(h * total_cols + ids_ref[1] * blocks + a, total_rows, total_cols) > 0
            keep = jnp.where(full, 0.5 + 0.5 * SHARE, 1.0)
            gain = jnp.where(full, 0.5, 0.0)
            turned = matmul(eye, square[b, :, 128 * i : 128 * (i + 1)], NT)
            out_ref[0, a] = keep * lag_ref[0, a].astype(F32) + gain * turned


def merge(ids, parts, offsets, markov, total_rows, total_cols):
    count = len(parts)
    halves, blocks, _, _ = markov.shape
    mm = 128 // count
    return pl.pallas_call(
        functools.partial(merge_kernel, tuple(offsets), total_rows, total_cols),
        out_shape=jax.ShapeDtypeStruct(markov.shape, F32),
        grid=(halves,),
        in_specs=[pl.BlockSpec(memory_space=pltpu.SMEM)]
        + [pl.BlockSpec((1, blocks // 2 * mm, 256), lambda h: (h, 0, 0))] * count
        + [pl.BlockSpec((1, blocks, 128, 128), lambda h: (h, 0, 0, 0))],
        out_specs=pl.BlockSpec((1, blocks, 128, 128), lambda h: (h, 0, 0, 0)),
        scratch_shapes=[pltpu.VMEM((blocks // 2, 128, 256), BF16)],
        compiler_params=pltpu.CompilerParams(vmem_limit_bytes=VMEM_LIMIT),
        name="merge",
    )(ids, *parts, markov)


def spread_rounds(count):
    rounds = [[(d, [0]) for d in (1, 2) if d < count]]
    have, shift = 3, 2
    while have < count:
        last = min(have + shift, count)
        rounds.append([(shift, list(range(have - shift, last - shift)))])
        have, shift = last, shift * 2
    return rounds


def spread_blocks(own, count, extra=None):
    got = {0: own}
    for number, step in enumerate(spread_rounds(count)):
        got.update({k + d: shift_col(got[k], d) for d, ks in step for k in ks})
        if extra is not None and number == 0:
            got, extra = lax.optimization_barrier((got, extra))
    return got, extra


def collect_blocks(far, middle, own, count):
    late = count // 2
    moved = shift_col(far, -late)
    middle = middle.astype(F32) + moved.astype(F32)
    total = {late - i: middle[i] for i in range(late)}
    total[0] = own.astype(F32)
    for step in reversed(spread_rounds(late + 1)):
        moved = [(k, shift_col(total[k + d].astype(BF16), -d)) for d, ks in step for k in ks]
        for k, block in moved:
            total[k] = total[k] + block.astype(F32)
    return total[0].astype(BF16)


def local(markov, omega):
    n_rows, n_cols = lax.axis_size("row"), lax.axis_size("col")
    r, c = lax.axis_index("row"), lax.axis_index("col")
    _, blocks, out_rows, columns = markov.shape
    rank = omega.shape[1]
    assert out_rows == 128 and columns == 128 and rank == 64 and n_rows >= 4
    kk, mm = rank // n_rows, columns // n_rows
    count = n_rows + 1
    pairs = blocks // 2
    rows = blocks * n_rows
    total_cols = blocks * n_cols
    distance = [count - 1 - e for e in range(count)]
    ids = jnp.stack([r, c]).astype(jnp.int32)

    own = omega.reshape(pairs, 2, columns, rank).transpose(0, 3, 1, 2).reshape(pairs, rank, 256)
    own = lax.dynamic_slice_in_dim(own, r * kk, kk, 1)
    lag_t = lax.dynamic_slice_in_dim(markov, r * mm, mm, 3)
    lag_t = lag_t.reshape(2, pairs, 2, out_rows, mm).transpose(0, 1, 4, 2, 3).reshape(2, pairs * mm, 256)
    got, lag_t = spread_blocks(own, count, lag_t)
    w_blocks = [got[d] for d in distance]

    late = count // 2
    partial = sketch_part(ids, markov, w_blocks, late, count - 1, rows)
    partial = sketch_part(ids, markov, w_blocks, 0, late, rows, partial)
    partial = lax.all_to_all(partial, "col", 0, 0, tiled=True)
    chunk = partial.reshape(n_cols, rows // n_cols, kk, 128).astype(F32).sum(0).astype(BF16)
    even = jnp.stack([chunk] + [shift_col(chunk, d) for d in range(2, n_cols, 2)])
    odd = swap("col", even, 1)
    sketches = gather_row(even)[0] + gather_row(odd)[0]

    basis, far = project(ids, sketches, lag_t, count)
    middle, mine = project_rest(ids, basis, lag_t, count, rank)
    mine = collect_blocks(far, middle, mine, count)
    got, _ = spread_blocks(mine, count)
    p_blocks = [got[d] for d in distance]

    sums = totals_near(ids, p_blocks, basis)
    part = totals_far(ids, p_blocks, basis, sums, lag_t)
    parts, offsets = gather_row(part)
    return merge(ids, parts, offsets, markov, rows, total_cols)


def solution(mesh):
    in_specs = (P(None, "col", None, None), P("col", None))
    out_specs = P(None, "col", None, None)
    return jax.shard_map(local, mesh=mesh, in_specs=in_specs, out_specs=out_specs, check_vma=False)
```
